32 devices in a mesh: pipe: 4 (over x, core), row: 4 (over z), col: 2 (over y).
Axes of the slice: x: 2, y: 2, z: 4, core: 2. Of those that a mesh axis runs over, the one named last changes fastest.
Arguments:
- handoff: bfloat16 [4, 256, 12288], P('pipe', 'col', 'row'), may hold values from -1200 to 1200
- norm_gain: float32 [4, 12288], P('pipe', 'row'), may hold values from 0.1 to 1.9
- norm_shift: float32 [4, 12288], P('pipe', 'row'), may hold values from -3 to 3
- up_weight: bfloat16 [4, 12288, 24576], P('pipe', 'row', 'col'), may hold values from -0.0546875 to 0.0546875
- up_bias: float32 [4, 24576], P('pipe', 'col'), may hold values from -3 to 3
Outputs:
- hidden: bfloat16 [4, 256, 24576], P('pipe', 'row', 'col')
The draws below stay inside these ranges and needn't reach their ends.
All inputs are finite; a program needn't handle non-finite values.
Results may differ from the reference program's by a relative error of at most 0.018.
Values may be sent and summed in bfloat16 or wider, within the bound.
A program may use at most 128 MiB of HBM per device.

```python
import math
import jax
import jax.numpy as jnp
from jax import lax

D = 12288
FF = 24576
MICRO = 256
SECTIONS = 4
FEATURE_BLOCKS = 4


def draw_handoff(key, part):
    key_rows, key_cols, key_jitter, key_offset = jax.random.split(key, 4)
    position = jnp.arange(D, dtype=jnp.float32) / D
    row_scale = jnp.exp(jax.random.uniform(key_rows, (SECTIONS, MICRO, 1), jnp.float32, 0.0, math.log(10.0)))
    feature_ramp = jnp.exp(math.log(3.0) * position)
    feature_spread = jnp.exp(jax.random.uniform(key_cols, (SECTIONS, 1, D), jnp.float32, 0.0, math.log(10.0)))
    jitter = jnp.clip(jax.random.normal(key_jitter, (SECTIONS, MICRO, D), jnp.float32), -3.0, 3.0)
    offset = jax.random.uniform(key_offset, (SECTIONS, MICRO, 1), jnp.float32, -1.0, 1.0)
    values = row_scale * feature_ramp * feature_spread * (jitter + offset)
    return values.astype(jnp.bfloat16)


def levels(own_key, shape, pieces, low, high):
    factor_of = 1.0
    for dim, parts in pieces:
        heights = jax.random.uniform(jax.random.fold_in(jax.random.fold_in(own_key, 6), dim), (parts,), jnp.float32, low / len(pieces), high / len(pieces))
        factor_of = factor_of * jnp.repeat(jnp.exp(heights), shape[dim] // parts).reshape((-1,) + (1,) * (len(shape) - 1 - dim))
    return factor_of


def normal_values(key, dims, deviation, bound, cuts=(), held_as=jnp.bfloat16):
    loudness = levels(key, dims, cuts, -0.22, 0.18) if cuts else 1.0
    drawn = jax.random.normal(key, dims, jnp.float32) * deviation * loudness
    return jnp.minimum(jnp.maximum(drawn, -bound), bound).astype(held_as)


def setup_inputs(seed: int = 0) -> dict:
    arg_keys = jax.random.split(jax.random.key(seed), 6)
    handoff = draw_handoff(jax.random.fold_in(arg_keys[5], 71), 0)
    norm_gain = jnp.clip(1.0 + 0.18 * jax.random.normal(arg_keys[1], (SECTIONS, D), jnp.float32), 0.1, 1.9)
    norm_shift = normal_values(arg_keys[2], (SECTIONS, D), 0.5, 3.0, ((0, 4), (1, 4)), jnp.float32)
    up_weight = normal_values(arg_keys[3], (SECTIONS, D, FF), D ** -0.5, 0.0546875, ((0, 4), (1, 4), (2, 2)))
    up_bias = normal_values(arg_keys[4], (SECTIONS, FF), 0.5, 3.0, ((0, 4), (1, 2)), jnp.float32)
    return dict(handoff=handoff, norm_gain=norm_gain, norm_shift=norm_shift, up_weight=up_weight, up_bias=up_bias)


epsilon = 1e-05

def one_section(inputs):
    arrived, norm_gain, norm_shift, up_weight, up_bias = inputs
    values = arrived.astype(jnp.float32)
    feature_count = values.shape[1]
    center = lax.optimization_barrier(jnp.sum(values, axis=1, keepdims=True)) / feature_count
    squares = lax.optimization_barrier(jnp.sum(values * values, axis=1, keepdims=True)) / feature_count
    inverse = lax.rsqrt(squares - center * center + epsilon)
    normed = ((values - center) * inverse * norm_gain + norm_shift).astype(jnp.bfloat16)
    block_width = feature_count // FEATURE_BLOCKS
    running = jnp.zeros((normed.shape[0], up_weight.shape[1]), jnp.float32)
    for block_index in range(FEATURE_BLOCKS):
        lower = block_index * block_width
        partial_value = jnp.dot(normed[:, lower:lower + block_width], up_weight[lower:lower + block_width], preferred_element_type=jnp.float32)
        rounded = lax.optimization_barrier(partial_value.astype(jnp.bfloat16))
        running = running + rounded.astype(jnp.float32)
    preact = running + up_bias
    return jax.nn.gelu(preact, approximate=True).astype(jnp.bfloat16)

def reference(handoff, norm_gain, norm_shift, up_weight, up_bias):
    arrived = jnp.roll(handoff, 1, axis=0)
    return lax.map(one_section, (arrived, norm_gain, norm_shift, up_weight, up_bias))
```

```python
import functools

import jax
import jax.numpy as jnp
from jax import lax
from jax.experimental import pallas as pl
from jax.experimental.pallas import tpu as pltpu
from jax.sharding import PartitionSpec as P

epsilon = 1e-05
MESH = pl.DeviceIdType.MESH
CHUNK = 1024
SUB = 512
SLOTS = 3


def section_kernel(
    stages, rows, cols,
    own_ref, gain_ref, shift_ref, weight_ref, bias_ref, out_ref,
    landed, stats_out, stats_in, normed, weights, partial, received,
    weight_sem, own_send, own_recv, stat_send, stat_recv, part_send, part_recv,
):
    pipe, me, col = lax.axis_index("pipe"), lax.axis_index("row"), lax.axis_index("col")
    after = lax.rem(pipe + 1, stages)
    before = lax.rem(pipe + stages - 1, stages)
    tokens, depth = own_ref.shape
    chunks, _, width = partial.shape
    per_group = rows // cols
    block = tokens // per_group
    feature_count = depth * rows
    steps = cols * chunks
    last = rows - 1

    def weight_copy(step):
        chunk, slot = lax.rem(step, chunks), lax.rem(step, SLOTS)
        columns = pl.ds(pl.multiple_of(chunk * width, width), width)
        return pltpu.make_async_copy(weight_ref.at[:, columns], weights.at[slot], weight_sem.at[slot])

    for step in range(min(SLOTS, steps)):
        weight_copy(step).start()

    barrier = pltpu.get_barrier_semaphore()

    def greet(i, carry):
        pl.semaphore_signal(
            barrier, inc=1, device_id=(before, i // cols, lax.rem(i, cols)), device_id_type=MESH
        )
        return carry

    lax.fori_loop(0, rows * cols, greet, 0)

    @pl.when(me > 0)
    def _():
        pl.semaphore_signal(barrier, inc=1, device_id=(pipe, me - 1, col), device_id_type=MESH)

    @pl.when(me < last)
    def _():
        pl.semaphore_signal(barrier, inc=1, device_id=(pipe, me + 1, col), device_id_type=MESH)

    values = own_ref[...].astype(jnp.float32)
    total = jnp.sum(values, axis=1, keepdims=True)
    squares = jnp.sum(values * values, axis=1, keepdims=True)
    lane = lax.broadcasted_iota(jnp.int32, (tokens, 128), 1)
    both = jnp.where(lane == 0, total, jnp.where(lane == 1, squares, 0.0))
    if tokens < 128:
        both = jnp.concatenate([both, jnp.zeros((128 - tokens, 128), jnp.float32)], axis=0)
    stats_out[...] = both.T[:8]

    neighbours = (me > 0).astype(jnp.int32) + (me < last).astype(jnp.int32)
    pl.semaphore_wait(barrier, rows * cols + neighbours)

    def own_copy(i):
        return pltpu.make_async_remote_copy(
            src_ref=own_ref, dst_ref=landed.at[col], send_sem=own_send.at[i], recv_sem=own_recv.at[col],
            device_id=(after, me, i), device_id_type=MESH,
        )

    def stat_copy(i):
        return pltpu.make_async_remote_copy(
            src_ref=stats_out, dst_ref=stats_in.at[col, me], send_sem=stat_send.at[i],
            recv_sem=stat_recv.at[col, me],
            device_id=(after, i // cols, lax.rem(i, cols)), device_id_type=MESH,
        )

    def start_stat(i, carry):
        stat_copy(i).start()
        return carry

    def start_own(i, carry):
        own_copy(lax.rem(col + i, cols)).start()
        return carry

    lax.fori_loop(0, rows * cols, start_stat, 0)
    lax.fori_loop(0, cols, start_own, 0)

    def to_normed(group):
        def wait_stat(z, carry):
            pltpu.make_async_remote_copy(
                src_ref=stats_out, dst_ref=stats_in.at[group, z], send_sem=stat_send.at[0],
                recv_sem=stat_recv.at[group, z], device_id=(after, me, col), device_id_type=MESH,
            ).wait_recv()
            return carry + stats_in[group, z]

        sums = lax.fori_loop(0, rows, wait_stat, jnp.zeros((8, 128), jnp.float32))
        by_token = jnp.concatenate([sums, jnp.zeros((120, 128), jnp.float32)], axis=0).T[:tokens]
        center = by_token[:, 0:1] / feature_count
        inverse = lax.rsqrt(by_token[:, 1:2] / feature_count - center * center + epsilon)
        pltpu.make_async_remote_copy(
            src_ref=own_ref, dst_ref=landed.at[group], send_sem=own_send.at[0],
            recv_sem=own_recv.at[group], device_id=(after, me, col), device_id_type=MESH,
        ).wait_recv()
        piece = 256
        for lower in range(0, depth, piece):
            part = landed[group, :, lower:lower + piece].astype(jnp.float32)
            scaled = (part - center) * inverse * gain_ref[:, lower:lower + piece]
            normed[:, lower:lower + piece] = (scaled + shift_ref[:, lower:lower + piece]).astype(jnp.bfloat16)

    def rows_of(b):
        return pl.ds(pl.multiple_of(b * block, block), block)

    def send(chunk, b, target, place):
        return pltpu.make_async_remote_copy(
            src_ref=partial.at[chunk, rows_of(b)], dst_ref=received.at[chunk, place],
            send_sem=part_send.at[chunk, b], recv_sem=part_recv.at[chunk, place],
            device_id=(pipe, target, col), device_id_type=MESH,
        )

    def arrival(chunk, b, place):
        send(chunk, b, me, place).wait_recv()
        return received[chunk, place].astype(jnp.float32)

    def group_of(phase):
        return lax.rem(col + phase, cols)

    def forward(chunk, b):
        @pl.when((b > me) & (me > 0))
        def _():
            own = partial[chunk, rows_of(b)].astype(jnp.float32)
            partial[chunk, rows_of(b)] = (own + arrival(chunk, b, b + 1)).astype(jnp.bfloat16)
            send(chunk, b, me + 1, b + 1).start()

        @pl.when((b < me) & (me < last))
        def _():
            own = partial[chunk, rows_of(b)].astype(jnp.float32)
            partial[chunk, rows_of(b)] = (own + arrival(chunk, b, b)).astype(jnp.bfloat16)
            send(chunk, b, me - 1, b).start()

        @pl.when(b == me)
        def _():
            @pl.when(me > 0)
            def _():
                send(chunk, b, me, b + 1).wait_recv()

            @pl.when(me < last)
            def _():
                send(chunk, b, me, b).wait_recv()

            columns = pl.ds(pl.multiple_of(chunk * width, width), width)
            preact = partial[chunk, rows_of(b)].astype(jnp.float32) + bias_ref[:, columns]
            left = jnp.where(me > 0, received[chunk, b + 1].astype(jnp.float32), 0.0)
            right = jnp.where(me < last, received[chunk, b].astype(jnp.float32), 0.0)
            preact = preact + left + right
            out_ref[:, columns] = jax.nn.gelu(preact, approximate=True).astype(jnp.bfloat16)

    def relay(index, carry):
        chunk, group = lax.rem(index, chunks), group_of(index // chunks)
        for i in range(per_group):
            forward(chunk, group * per_group + i)
        return carry

    inner = (me > 0) & (me < last)

    def phase_body(phase, carry):
        group = group_of(phase)
        to_normed(group)

        def chunk_body(chunk, carry):
            step = phase * chunks + chunk
            slot = lax.rem(step, SLOTS)
            weight_copy(step).wait()
            lines = pl.ds(pl.multiple_of(group * tokens, tokens), tokens)
            for lower in range(0, width, SUB):
                product = jnp.dot(
                    normed[...], weights[slot, :, lower:lower + SUB], preferred_element_type=jnp.float32
                )
                partial[chunk, lines, lower:lower + SUB] = product.astype(jnp.bfloat16)

            @pl.when(step + SLOTS < steps)
            def _():
                weight_copy(step + SLOTS).start()

            for i in range(per_group):
                b = group * per_group + per_group - 1 - i

                @pl.when((me == 0) & (b > 0))
                def _():
                    send(chunk, b, me + 1, b + 1).start()

            for i in range(per_group):
                b = group * per_group + i

                @pl.when((me == last) & (b < last))
                def _():
                    send(chunk, b, me - 1, b).start()

            late = step - chunks

            @pl.when(inner & (late >= 0) & (lax.rem(late + chunks, 2) == 0))
            def _():
                relay(late // 2, 0)

            return carry

        return lax.fori_loop(0, chunks, chunk_body, carry)

    lax.fori_loop(0, cols, phase_body, 0)
    done = len([late for late in range(steps - chunks) if (late + chunks) % 2 == 0])
    lax.fori_loop(jnp.where(inner, done, 0), steps, relay, 0)

    def finish(i, carry):
        chunk, b = i // rows, lax.rem(i, rows)

        @pl.when(b != me)
        def _():
            send(chunk, b, me, b).wait_send()

        return carry

    lax.fori_loop(0, chunks * rows, finish, 0)

    def finish_stat(i, carry):
        stat_copy(i).wait_send()
        return carry

    def finish_own(i, carry):
        own_copy(i).wait_send()
        return carry

    lax.fori_loop(0, rows * cols, finish_stat, 0)
    lax.fori_loop(0, cols, finish_own, 0)


def local(stages, rows, cols, handoff, norm_gain, norm_shift, up_weight, up_bias):
    own = handoff[0]
    tokens, depth = own.shape
    hidden = up_weight.shape[2]
    width = min(CHUNK, hidden)
    chunks = hidden // width
    micro = tokens * cols
    block = micro // rows
    vmem = pl.BlockSpec(memory_space=pltpu.VMEM)
    result = pl.pallas_call(
        functools.partial(section_kernel, stages, rows, cols),
        out_shape=jax.ShapeDtypeStruct((block, hidden), jnp.bfloat16),
        in_specs=[vmem, vmem, vmem, pl.BlockSpec(memory_space=pl.ANY), vmem],
        out_specs=vmem,
        scratch_shapes=[
            pltpu.VMEM((cols, tokens, depth), jnp.bfloat16),
            pltpu.VMEM((8, 128), jnp.float32),
            pltpu.VMEM((cols, rows, 8, 128), jnp.float32),
            pltpu.VMEM((tokens, depth), jnp.bfloat16),
            pltpu.VMEM((SLOTS, depth, width), jnp.bfloat16),
            pltpu.VMEM((chunks, micro, width), jnp.bfloat16),
            pltpu.VMEM((chunks, rows + 1, block, width), jnp.bfloat16),
            pltpu.SemaphoreType.DMA((SLOTS,)),
            pltpu.SemaphoreType.DMA((cols,)),
            pltpu.SemaphoreType.DMA((cols,)),
            pltpu.SemaphoreType.DMA((rows * cols,)),
            pltpu.SemaphoreType.DMA((cols, rows)),
            pltpu.SemaphoreType.DMA((chunks, rows)),
            pltpu.SemaphoreType.DMA((chunks, rows + 1)),
        ],
        compiler_params=pltpu.CompilerParams(
            collective_id=0, has_side_effects=True, vmem_limit_bytes=60 * 1024 * 1024
        ),
    )(own, norm_gain, norm_shift, up_weight[0], up_bias)
    return result[None]


def solution(mesh):
    in_specs = (
        P("pipe", "col", "row"),
        P("pipe", "row"),
        P("pipe", "row"),
        P("pipe", "row", "col"),
        P("pipe", "col"),
    )
    out_specs = P("pipe", "row", "col")
    sizes = mesh.shape["pipe"], mesh.shape["row"], mesh.shape["col"]
    return jax.shard_map(
        functools.partial(local, *sizes), mesh=mesh, in_specs=in_specs, out_specs=out_specs, check_vma=False
    )
```

```python
import functools

import jax
import jax.numpy as jnp
from jax import lax
from jax.experimental import pallas as pl
from jax.experimental.pallas import tpu as pltpu
from jax.sharding import PartitionSpec as P

epsilon = 1e-05
MESH = pl.DeviceIdType.MESH
CHUNK = 1024
SUB = 512
SLOTS = 3
LAG = 2


def section_kernel(
    stages, rows, cols,
    own_ref, gain_ref, shift_ref, weight_ref, bias_ref, out_ref,
    landed, stats_out, stats_in, normed, weights, partial, received,
    weight_sem, own_send, own_recv, stat_send, stat_recv, part_send, part_recv,
):
    pipe, me, col = lax.axis_index("pipe"), lax.axis_index("row"), lax.axis_index("col")
    after = lax.rem(pipe + 1, stages)
    before = lax.rem(pipe + stages - 1, stages)
    tokens, depth = own_ref.shape
    chunks, _, width = partial.shape
    per_group = rows // cols
    block = tokens // per_group
    feature_count = depth * rows
    steps = cols * chunks
    last = rows - 1

    def weight_copy(step):
        chunk, slot = lax.rem(step, chunks), lax.rem(step, SLOTS)
        columns = pl.ds(pl.multiple_of(chunk * width, width), width)
        return pltpu.make_async_copy(weight_ref.at[:, columns], weights.at[slot], weight_sem.at[slot])

    for step in range(min(SLOTS, steps)):
        weight_copy(step).start()

    barrier = pltpu.get_barrier_semaphore()

    def greet(i, carry):
        pl.semaphore_signal(
            barrier, inc=1, device_id=(before, i // cols, lax.rem(i, cols)), device_id_type=MESH
        )
        return carry

    lax.fori_loop(0, rows * cols, greet, 0)

    @pl.when(me > 0)
    def _():
        pl.semaphore_signal(barrier, inc=1, device_id=(pipe, me - 1, col), device_id_type=MESH)

    @pl.when(me < last)
    def _():
        pl.semaphore_signal(barrier, inc=1, device_id=(pipe, me + 1, col), device_id_type=MESH)

    values = own_ref[...].astype(jnp.float32)
    total = jnp.sum(values, axis=1, keepdims=True)
    squares = jnp.sum(values * values, axis=1, keepdims=True)
    lane = lax.broadcasted_iota(jnp.int32, (tokens, 128), 1)
    both = jnp.where(lane == 0, total, jnp.where(lane == 1, squares, 0.0))
    if tokens < 128:
        both = jnp.concatenate([both, jnp.zeros((128 - tokens, 128), jnp.float32)], axis=0)
    stats_out[...] = both.T[:8]

    neighbours = (me > 0).astype(jnp.int32) + (me < last).astype(jnp.int32)
    pl.semaphore_wait(barrier, rows * cols + neighbours)

    def own_copy(i):
        return pltpu.make_async_remote_copy(
            src_ref=own_ref, dst_ref=landed.at[col], send_sem=own_send.at[i], recv_sem=own_recv.at[col],
            device_id=(after, me, i), device_id_type=MESH,
        )

    def stat_copy(i):
        return pltpu.make_async_remote_copy(
            src_ref=stats_out, dst_ref=stats_in.at[col, me], send_sem=stat_send.at[i],
            recv_sem=stat_recv.at[col, me],
            device_id=(after, i // cols, lax.rem(i, cols)), device_id_type=MESH,
        )

    def start_stat(i, carry):
        stat_copy(i).start()
        return carry

    def start_own(i, carry):
        own_copy(lax.rem(col + i, cols)).start()
        return carry

    lax.fori_loop(0, rows * cols, start_stat, 0)
    lax.fori_loop(0, cols, start_own, 0)

    def to_normed(group):
        def wait_stat(z, carry):
            pltpu.make_async_remote_copy(
                src_ref=stats_out, dst_ref=stats_in.at[group, z], send_sem=stat_send.at[0],
                recv_sem=stat_recv.at[group, z], device_id=(after, me, col), device_id_type=MESH,
            ).wait_recv()
            return carry + stats_in[group, z]

        sums = lax.fori_loop(0, rows, wait_stat, jnp.zeros((8, 128), jnp.float32))
        by_token = jnp.concatenate([sums, jnp.zeros((120, 128), jnp.float32)], axis=0).T[:tokens]
        center = by_token[:, 0:1] / feature_count
        inverse = lax.rsqrt(by_token[:, 1:2] / feature_count - center * center + epsilon)
        pltpu.make_async_remote_copy(
            src_ref=own_ref, dst_ref=landed.at[group], send_sem=own_send.at[0],
            recv_sem=own_recv.at[group], device_id=(after, me, col), device_id_type=MESH,
        ).wait_recv()
        piece = 256
        for lower in range(0, depth, piece):
            part = landed[group, :, lower:lower + piece].astype(jnp.float32)
            scaled = (part - center) * inverse * gain_ref[:, lower:lower + piece]
            normed[:, lower:lower + piece] = (scaled + shift_ref[:, lower:lower + piece]).astype(jnp.bfloat16)

    def rows_of(b):
        return pl.ds(pl.multiple_of(b * block, block), block)

    def send(chunk, b, target, place):
        return pltpu.make_async_remote_copy(
            src_ref=partial.at[chunk, rows_of(b)], dst_ref=received.at[chunk, place],
            send_sem=part_send.at[chunk, b], recv_sem=part_recv.at[chunk, place],
            device_id=(pipe, target, col), device_id_type=MESH,
        )

    def arrival(chunk, b, place):
        send(chunk, b, me, place).wait_recv()
        return received[chunk, place].astype(jnp.float32)

    def group_of(phase):
        return lax.rem(col + phase, cols)

    def pass_on(chunk, b):
        @pl.when((b > me) & (me > 0))
        def _():
            own = partial[chunk, rows_of(b)].astype(jnp.float32)
            partial[chunk, rows_of(b)] = (own + arrival(chunk, b, b + 1)).astype(jnp.bfloat16)
            send(chunk, b, me + 1, b + 1).start()

        @pl.when((b < me) & (me < last))
        def _():
            own = partial[chunk, rows_of(b)].astype(jnp.float32)
            partial[chunk, rows_of(b)] = (own + arrival(chunk, b, b)).astype(jnp.bfloat16)
            send(chunk, b, me - 1, b).start()

    def conclude(chunk, b):
        @pl.when(b == me)
        def _():
            @pl.when(me > 0)
            def _():
                send(chunk, b, me, b + 1).wait_recv()

            @pl.when(me < last)
            def _():
                send(chunk, b, me, b).wait_recv()

            columns = pl.ds(pl.multiple_of(chunk * width, width), width)
            preact = partial[chunk, rows_of(b)].astype(jnp.float32) + bias_ref[:, columns]
            left = jnp.where(me > 0, received[chunk, b + 1].astype(jnp.float32), 0.0)
            right = jnp.where(me < last, received[chunk, b].astype(jnp.float32), 0.0)
            preact = preact + left + right
            out_ref[:, columns] = jax.nn.gelu(preact, approximate=True).astype(jnp.bfloat16)

    def relay(index, carry):
        chunk, group = lax.rem(index, chunks), group_of(index // chunks)
        for i in range(per_group):
            pass_on(chunk, group * per_group + i)
        return carry

    def final(index, carry):
        chunk, group = lax.rem(index, chunks), group_of(index // chunks)
        for i in range(per_group):
            conclude(chunk, group * per_group + i)
        return carry

    half = chunks // 2
    paced = cols == 2 and rows == 4 and chunks % 2 == 0
    first_leads = lax.rem(me + col, 2) == 0

    def pace(turn, carry):
        one = turn - jnp.where(first_leads, 0, LAG)
        two = turn - half - jnp.where(first_leads, LAG, 0)

        @pl.when((one >= 0) & (one < chunks))
        def _():
            relay(one, 0)

        @pl.when((two >= 0) & (two < chunks))
        def _():
            relay(chunks + two, 0)

        for i in range(2):
            @pl.when((turn >= chunks) & (turn < chunks + half))
            def _():
                final(2 * (turn - chunks) + i, 0)

            @pl.when(turn >= chunks + LAG)
            def _():
                final(chunks + 2 * (turn - chunks - LAG) + i, 0)

        return carry

    inner = (me > 0) & (me < last)

    def phase_body(phase, carry):
        group = group_of(phase)
        to_normed(group)

        def chunk_body(chunk, carry):
            step = phase * chunks + chunk
            slot = lax.rem(step, SLOTS)
            weight_copy(step).wait()
            lines = pl.ds(pl.multiple_of(group * tokens, tokens), tokens)
            for lower in range(0, width, SUB):
                product = jnp.dot(
                    normed[...], weights[slot, :, lower:lower + SUB], preferred_element_type=jnp.float32
                )
                partial[chunk, lines, lower:lower + SUB] = product.astype(jnp.bfloat16)

            @pl.when(step + SLOTS < steps)
            def _():
                weight_copy(step + SLOTS).start()

            for i in range(per_group):
                b = group * per_group + per_group - 1 - i

                @pl.when((me == 0) & (b > 0))
                def _():
                    send(chunk, b, me + 1, b + 1).start()

            for i in range(per_group):
                b = group * per_group + i

                @pl.when((me == last) & (b < last))
                def _():
                    send(chunk, b, me - 1, b).start()

            late = step - chunks

            @pl.when(inner & (late >= 0) & (lax.rem(late + chunks, 2) == 0))
            def _():
                pace(late // 2, 0) if paced else relay(late // 2, 0)

            return carry

        return lax.fori_loop(0, chunks, chunk_body, carry)

    lax.fori_loop(0, cols, phase_body, 0)
    done = len([late for late in range(steps - chunks) if (late + chunks) % 2 == 0])

    @pl.when(inner)
    def _():
        if paced:
            lax.fori_loop(half, chunks + half + LAG, pace, 0)
        else:
            lax.fori_loop(done, steps, relay, 0)
            lax.fori_loop(0, steps, final, 0)

    @pl.when(jnp.logical_not(inner))
    def _():
        lax.fori_loop(0, steps, final, 0)

    def finish(i, carry):
        chunk, b = i // rows, lax.rem(i, rows)

        @pl.when(b != me)
        def _():
            send(chunk, b, me, b).wait_send()

        return carry

    lax.fori_loop(0, chunks * rows, finish, 0)

    def finish_stat(i, carry):
        stat_copy(i).wait_send()
        return carry

    def finish_own(i, carry):
        own_copy(i).wait_send()
        return carry

    lax.fori_loop(0, rows * cols, finish_stat, 0)
    lax.fori_loop(0, cols, finish_own, 0)


def local(stages, rows, cols, handoff, norm_gain, norm_shift, up_weight, up_bias):
    own = handoff[0]
    tokens, depth = own.shape
    hidden = up_weight.shape[2]
    width = min(CHUNK, hidden)
    chunks = hidden // width
    micro = tokens * cols
    block = micro // rows
    vmem = pl.BlockSpec(memory_space=pltpu.VMEM)
    result = pl.pallas_call(
        functools.partial(section_kernel, stages, rows, cols),
        out_shape=jax.ShapeDtypeStruct((block, hidden), jnp.bfloat16),
        in_specs=[vmem, vmem, vmem, pl.BlockSpec(memory_space=pl.ANY), vmem],
        out_specs=vmem,
        scratch_shapes=[
            pltpu.VMEM((cols, tokens, depth), jnp.bfloat16),
            pltpu.VMEM((8, 128), jnp.float32),
            pltpu.VMEM((cols, rows, 8, 128), jnp.float32),
            pltpu.VMEM((tokens, depth), jnp.bfloat16),
            pltpu.VMEM((SLOTS, depth, width), jnp.bfloat16),
            pltpu.VMEM((chunks, micro, width), jnp.bfloat16),
            pltpu.VMEM((chunks, rows + 1, block, width), jnp.bfloat16),
            pltpu.SemaphoreType.DMA((SLOTS,)),
            pltpu.SemaphoreType.DMA((cols,)),
            pltpu.SemaphoreType.DMA((cols,)),
            pltpu.SemaphoreType.DMA((rows * cols,)),
            pltpu.SemaphoreType.DMA((cols, rows)),
            pltpu.SemaphoreType.DMA((chunks, rows)),
            pltpu.SemaphoreType.DMA((chunks, rows + 1)),
        ],
        compiler_params=pltpu.CompilerParams(
            collective_id=0, has_side_effects=True, vmem_limit_bytes=60 * 1024 * 1024
        ),
    )(own, norm_gain, norm_shift, up_weight[0], up_bias)
    return result[None]


def solution(mesh):
    in_specs = (
        P("pipe", "col", "row"),
        P("pipe", "row"),
        P("pipe", "row"),
        P("pipe", "row", "col"),
        P("pipe", "col"),
    )
    out_specs = P("pipe", "row", "col")
    sizes = mesh.shape["pipe"], mesh.shape["row"], mesh.shape["col"]
    return jax.shard_map(
        functools.partial(local, *sizes), mesh=mesh, in_specs=in_specs, out_specs=out_specs, check_vma=False
    )
```
